512 devices in a mesh: rep: 64 (over x, y, core), mp: 8 (over z).
Axes of the slice: x: 4, y: 8, z: 8, core: 2. Of those that a mesh axis runs over, the one named last changes fastest.
Arguments:
- tokens_in: bfloat16 [16384, 8192], P('rep', 'mp'), may hold values from -2100 to 2100
- norm_gain: bfloat16 [8192], P('mp'), may hold values from 0.5 to 1.5
- key_grad: bfloat16 [16384, 512], P('rep'), may hold values from -1 to 1
- error_in: float32 [64, 8192, 512], P('rep', 'mp'), may hold values from -6 to 6
- basis_init: float32 [512, 128], P('mp'), may hold values from -6 to 6
- weights_in: float32 [8, 1024, 512], P('mp', 'rep'), may hold values from -0.75 to 0.75
- momentum_in: float32 [8, 1024, 512], P('mp', 'rep'), may hold values from -1.5 to 1.5
Outputs:
- error_out: float32 [64, 8192, 512], P('rep', 'mp')
- weights_out: float32 [8, 1024, 512], P('mp', 'rep')
- momentum_out: float32 [8, 1024, 512], P('mp', 'rep')
The draws below stay inside these ranges and needn't reach their ends.
All inputs are finite; a program needn't handle non-finite values.
Results may differ from the reference program's by a relative error of at most 0.0025.
Values sent between devices are 32-bit elements; how exact they have to be, the bound alone decides.
A program may use at most 64 MiB of HBM per device.

```python
import math
import jax
import jax.numpy as jnp
from jax import lax

D = 8192
RANK = 128
ITERS = 2
TOK = 256
KW = 512
DL = 1024
ALLTOK = 16384
N_REP = 64
N_MP = 8


def draw_tokens_in(key, part):
    first, second, third = jax.random.split(key, 3)
    row_scales = jnp.exp(jax.random.uniform(first, (ALLTOK, 1), jnp.float32) * math.log(10.0))
    column_scales = jnp.exp(jax.random.uniform(second, (1, D), jnp.float32) * math.log(10.0))
    rising = jnp.exp(jnp.arange(D, dtype=jnp.float32)[None, :] / D * math.log(3.0))
    values = jnp.clip(jax.random.normal(third, (ALLTOK, D), jnp.float32), -6.0, 6.0)
    return (values * row_scales * column_scales * rising).astype(jnp.bfloat16)


def shard_levels(key, dims, cuts, low, top_value):
    factor_of, own = 1.0, jax.random.fold_in(key, 6)
    for dim, blocks in cuts:
        draws = jnp.exp(jax.random.uniform(jax.random.fold_in(own, dim), (blocks,), jnp.float32, low / len(cuts), top_value / len(cuts)))
        factor_of = factor_of * jnp.repeat(draws, dims[dim] // blocks).reshape([-1 if axis == dim else 1 for axis in range(len(dims))])
    return factor_of


def centred(own_key, extent, deviation, bound, shards=(), held_as=jnp.bfloat16):
    result = deviation * jax.random.normal(own_key, extent, jnp.float32)
    if shards:
        result = result * shard_levels(own_key, extent, shards, -0.22, 0.18)
    return jnp.clip(result, -bound, bound).astype(held_as)


def setup_inputs(seed: int = 0) -> dict:
    keys = jax.random.split(jax.random.key(seed), 8)
    tokens_in = draw_tokens_in(jax.random.fold_in(keys[7], 71), 0)
    norm_gain = jnp.clip(1.0 + 0.1 * jax.random.normal(keys[1], (D,), jnp.float32), 0.5, 1.5).astype(jnp.bfloat16)
    key_grad = centred(keys[2], (ALLTOK, KW), (TOK ** -0.5), 1.0, ((0, 64),))
    error_in = centred(keys[3], (N_REP, D, KW), 1.0, 6.0, ((0, 64), (1, 8)), jnp.float32)
    basis_init = centred(keys[4], (KW, RANK), 1.0, 6.0, ((0, 8),), jnp.float32)
    weights_in = centred(keys[5], (N_MP, DL, KW), 0.05, 0.75, ((0, 8), (1, 64)), jnp.float32)
    momentum_in = centred(keys[6], (N_MP, DL, KW), 0.1, 1.5, ((0, 8), (1, 64)), jnp.float32)
    return {"tokens_in": tokens_in, "norm_gain": norm_gain, "key_grad": key_grad, "error_in": error_in, "basis_init": basis_init, "weights_in": weights_in, "momentum_in": momentum_in}


precise = lax.Precision.HIGHEST
epsilon = 1e-05
momentum_rate = 0.9
outer_rate = 0.7

def right_solve(lower_factor, row_block):
    return jax.scipy.linalg.solve_triangular(lower_factor, row_block.T, lower=True).T

def reference(tokens_in, norm_gain, key_grad, error_in, basis_init, weights_in, momentum_in):
    widened = tokens_in.astype(jnp.float32)
    mean_square = lax.optimization_barrier(jnp.mean(widened * widened, axis=1, keepdims=True))
    normed = (widened * lax.rsqrt(mean_square + epsilon) * norm_gain.astype(jnp.float32)[None, :]).astype(jnp.bfloat16)
    normed_wide = normed.astype(jnp.float32).reshape(N_REP, TOK, D)
    cotangents = key_grad.astype(jnp.float32).reshape(N_REP, TOK, KW)
    weight_change = jnp.einsum('rtd,rtk->rdk', normed_wide, cotangents, precision=precise)
    merged = weight_change + error_in
    right_factor = basis_init
    orthonormal = jnp.zeros((D, RANK), jnp.float32)
    for iteration in range(ITERS):
        left_factor = jnp.einsum('rdk,kq->dq', merged, right_factor, precision=precise) / N_REP
        gram_matrix = jnp.dot(left_factor.T, left_factor, precision=precise)
        lower_factor = jnp.linalg.cholesky(gram_matrix)
        orthonormal = right_solve(lower_factor, left_factor)
        right_factor = jnp.einsum('rdk,dq->kq', merged, orthonormal, precision=precise) / N_REP
    approximant = jnp.dot(orthonormal, right_factor.T, precision=precise)
    error_out = merged - approximant[None]
    approx_rows = approximant.reshape(N_MP, D // N_MP, KW)
    momentum_out = momentum_rate * momentum_in + approx_rows
    weights_out = weights_in - outer_rate * (approx_rows + momentum_rate * momentum_out)
    return (error_out, weights_out, momentum_out)
```

```python
import functools

import jax
import jax.numpy as jnp
from jax import lax
from jax.experimental import pallas as pl
from jax.experimental.pallas import tpu as pltpu
from jax.sharding import PartitionSpec as P

D = 8192
CORES = 2
SHAPE = (4, 8)
MESH = pl.DeviceIdType.MESH
F32 = jnp.float32
HI = lax.Precision.HIGHEST
EPS = 1e-5
MOMENTUM = 0.9
RATE = 0.7


def dot(a, b, dims, precision=HI):
    return lax.dot_general(a, b, (dims, ((), ())), precision=precision, preferred_element_type=F32)


NN = ((1,), (0,))
TN = ((0,), (0,))
NT = ((1,), (1,))


def exchange_kernel(
    nx, ny, nz,
    tok_h, gain_ref, kg_h, err_h, basis_ref,
    merged_h, mean_ref, gram_ref, full_ref,
    tok, kg, err, nrm, mg, cx, hs,
    sq, m0a, m0b, m1a, m1b, part, rows, gh, g0a, g0b, g1a, g1b, gpart, gz,
    local_sem, ssem, rsem,
):
    me = lax.axis_index("rep")
    z = lax.axis_index("mp")
    core = lax.rem(me, 2)
    y = lax.rem(lax.div(me, 2), ny)
    x = lax.div(me, 2 * ny)
    reps = nx * ny * CORES
    dl, kw = mg.shape
    half = dl // 2
    ghalf = kw // 2

    def at(xx, yy, cc, zz):
        return ((xx * ny + yy) * 2 + cc, zz)

    partner = at(x, y, 1 - core, z)
    xs = [None] + [at(lax.rem(x + d, nx), y, core, z) for d in range(1, nx)]
    ys = [None] + [at(x, lax.rem(y + d, ny), core, z) for d in range(1, ny)]
    zs = [None] + [at(x, y, core, lax.rem(z + d, nz)) for d in range(1, nz)]

    loads = [
        pltpu.make_async_copy(tok_h, tok, local_sem.at[0]),
        pltpu.make_async_copy(kg_h, kg, local_sem.at[1]),
        pltpu.make_async_copy(err_h.at[0], err, local_sem.at[2]),
    ]
    for load in loads:
        load.start()
    barrier = pltpu.get_barrier_semaphore()
    peers = [partner] + xs[1:] + ys[1:] + zs[1:]
    for peer in peers:
        pl.semaphore_signal(barrier, inc=1, device_id=peer, device_id_type=MESH)

    count = [0]

    def ids(n):
        first = count[0]
        count[0] += n
        return first

    def copy(src, dst, k, dev):
        return pltpu.make_async_remote_copy(
            src_ref=src, dst_ref=dst, send_sem=ssem.at[k], recv_sem=rsem.at[k], device_id=dev, device_id_type=MESH
        )

    def start(copies):
        for c in copies:
            c.start()

    def arrive(copies):
        for c in copies:
            c.wait_recv()

    def sent(copies):
        for c in copies:
            c.wait_send()

    loads[0].wait()
    acc = jnp.zeros((tok.shape[0], 128), F32)
    for b in range(dl // 128):
        t = tok[:, b * 128:(b + 1) * 128].astype(F32)
        acc = acc + t * t
    sq[0] = jnp.sum(acc.T, axis=0, keepdims=True)
    zb = basis_ref.shape[0]
    full_ref[pl.ds(pl.multiple_of(z * zb, zb), zb), :] = basis_ref[...]
    pl.semaphore_wait(barrier, len(peers))

    k = ids(nz)
    sq_copies = [copy(sq.at[0], sq.at[d], k + d, zs[d]) for d in range(1, nz)]
    start(sq_copies)
    k = ids(nz)
    mine = full_ref.at[pl.ds(pl.multiple_of(z * zb, zb), zb), :]
    basis_copies = [copy(basis_ref, mine, k + d, zs[d]) for d in range(1, nz)]
    start(basis_copies)
    arrive(sq_copies)
    total = sq[0]
    for d in range(1, nz):
        total = total + sq[d]
    scale = lax.rsqrt(total / D + EPS)
    scale = jnp.broadcast_to(scale, (128, scale.shape[1])).T
    for b in range(dl // 128):
        cols = slice(b * 128, (b + 1) * 128)
        t = tok[:, cols].astype(F32) * scale * gain_ref[:, cols].astype(F32)
        nrm[:, cols] = t.astype(jnp.bfloat16)
    loads[1].wait()
    loads[2].wait()

    step = half // 2
    k = ids(2)
    pair_copies = []

    def merge(first):
        first = pl.multiple_of(first, step)
        w = dot(nrm[:, pl.ds(first, step)], kg[...], TN, None)
        mg[pl.ds(first, step), :] = w + err[pl.ds(first, step), :]

    for i in range(2):
        first = pl.multiple_of((1 - core) * half + i * step, step)
        merge(first)
        c = copy(mg.at[pl.ds(first, step), :], cx.at[pl.ds(i * step, step), :], k + i, partner)
        c.start()
        pair_copies.append(c)
    for i in range(2):
        merge(core * half + i * step)
    store = pltpu.make_async_copy(mg, merged_h, local_sem.at[3])
    store.start()
    for i in range(2):
        pair_copies[i].wait_recv()
        own = pl.ds(pl.multiple_of(core * half + i * step, step), step)
        hs[i * step:(i + 1) * step, :] = mg[own, :] + cx[i * step:(i + 1) * step, :]

    def scatter(src, base, size, slots, peers, place, n, k):
        out = []
        for d in range(1, n):
            target = lax.rem(place + d, n)
            first = pl.multiple_of(base + target * size, size)
            out.append(copy(src.at[pl.ds(first, size), :], slots.at[d], k + d, peers[d]))
        return out

    def gathered(src, base, size, slots, place, n):
        v = src[pl.ds(pl.multiple_of(base + place * size, size), size), :]
        for d in range(1, n):
            v = v + slots[d]
        return v

    big = max(nx, ny)
    ka, kb = ids(big), ids(big)
    rp = half // (nx * ny)
    row = pl.multiple_of(jnp.where(core == 0, (x * ny + y) * rp, half + (y * nx + x) * rp), rp)

    def plane(src, part, a0, b0, a1, b1, piece, ka, kb, put):
        @pl.when(core == 0)
        def _():
            first = scatter(src, 0, ny * piece, a0, xs, x, nx, ka)
            start(first)
            arrive(first)
            part[pl.ds(0, ny * piece), :] = gathered(src, 0, ny * piece, a0, x, nx)
            second = scatter(part, 0, piece, b0, ys, y, ny, kb)
            start(second)
            arrive(second)
            put(gathered(part, 0, piece, b0, y, ny))
            sent(first)
            sent(second)

        @pl.when(core == 1)
        def _():
            first = scatter(src, 0, nx * piece, a1, ys, y, ny, ka)
            start(first)
            arrive(first)
            part[pl.ds(0, nx * piece), :] = gathered(src, 0, nx * piece, a1, y, ny)
            second = scatter(part, 0, piece, b1, xs, x, nx, kb)
            start(second)
            arrive(second)
            put(gathered(part, 0, piece, b1, x, nx))
            sent(first)
            sent(second)

    def put_rows(v):
        v = v * (1.0 / reps)
        mean_ref[pl.ds(row, rp), :] = v
        rows[0] = v

    plane(hs, part, m0a, m0b, m1a, m1b, rp, ka, kb, put_rows)

    k = ids(1)
    row_copy = copy(rows.at[0], rows.at[1], k, partner)
    row_copy.start()

    def spread(ref, base0, base1, piece, ka, kb):
        def block(first, size):
            return ref.at[pl.ds(pl.multiple_of(first, size), size), :]

        def along(first, size, peers, n, k):
            return [copy(block(first, size), block(first, size), k + d, peers[d]) for d in range(1, n)]

        one0 = along(base0 + (x * ny + y) * piece, piece, ys, ny, ka)
        two0 = along(base0 + x * ny * piece, ny * piece, xs, nx, kb)
        one1 = along(base1 + (y * nx + x) * piece, piece, xs, nx, ka)
        two1 = along(base1 + y * nx * piece, nx * piece, ys, ny, kb)
        return one0, two0, one1, two1

    def by_core(zero, one, act):
        @pl.when(core == 0)
        def _():
            act(zero)

        @pl.when(core == 1)
        def _():
            act(one)

    mean_one0, mean_two0, mean_one1, mean_two1 = spread(mean_ref, 0, half, rp, ids(big), ids(big))
    by_core(mean_one0, mean_one1, start)

    row_copy.wait_recv()
    both = rows[...].reshape(2 * rp, kw)
    lhs = rows[:, :, pl.ds(pl.multiple_of(core * ghalf, ghalf), ghalf)].reshape(2 * rp, ghalf)
    gh[...] = dot(lhs, both, TN)
    gp = ghalf // (nx * ny)
    grow = pl.multiple_of(jnp.where(core == 0, (x * ny + y) * gp, ghalf + (y * nx + x) * gp), gp)

    def put_gram(v):
        gz[0] = v

    plane(gh, gpart, g0a, g0b, g1a, g1b, gp, ids(big), ids(big), put_gram)
    k = ids(nz)
    z_copies = [copy(gz.at[0], gz.at[d], k + d, zs[d]) for d in range(1, nz)]
    start(z_copies)
    by_core(mean_one0, mean_one1, arrive)
    by_core(mean_two0, mean_two1, start)
    arrive(z_copies)
    v = gz[0]
    for d in range(1, nz):
        v = v + gz[d]
    gram_ref[pl.ds(grow, gp), :] = v

    gram_one0, gram_two0, gram_one1, gram_two1 = spread(gram_ref, 0, ghalf, gp, ids(big), ids(big))
    by_core(gram_one0, gram_one1, start)
    by_core(gram_one0, gram_one1, arrive)
    by_core(gram_two0, gram_two1, start)
    by_core(gram_two0, gram_two1, arrive)

    def swap(ref, size, k):
        own = ref.at[pl.ds(pl.multiple_of(core * size, size), size), :]
        return copy(own, own, k, partner)

    gram_swap = swap(gram_ref, ghalf, ids(1))
    gram_swap.start()
    by_core(mean_two0, mean_two1, arrive)
    mean_swap = swap(mean_ref, half, ids(1))
    mean_swap.start()
    arrive(basis_copies)
    gram_swap.wait_recv()
    mean_swap.wait_recv()
    store.wait()
    sent(sq_copies + basis_copies + pair_copies + [row_copy] + z_copies + [gram_swap, mean_swap])
    by_core(mean_one0, mean_one1, sent)
    by_core(mean_two0, mean_two1, sent)
    by_core(gram_one0, gram_one1, sent)
    by_core(gram_two0, gram_two1, sent)


def inverse_factor(a):
    n = a.shape[0]
    groups = n // 8
    left = [a[8 * g:8 * g + 8, :] for g in range(groups)]
    row_id = lax.broadcasted_iota(jnp.int32, (8, n), 0)
    lane_id = lax.broadcasted_iota(jnp.int32, (8, n), 1)
    right = [jnp.where(lane_id == row_id + 8 * g, 1.0, 0.0).astype(F32) for g in range(groups)]
    done = list(right)
    for j in range(n):
        g, i = divmod(j, 8)
        pivot_row = jnp.broadcast_to(left[g][i:i + 1, :], (8, n))
        pivot = jnp.broadcast_to(pivot_row[:, j:j + 1], (8, n))
        inv = 1.0 / pivot
        unit = jnp.broadcast_to(right[g][i:i + 1, :], (8, n))
        done[g] = jnp.where(row_id == i, unit * lax.rsqrt(pivot), done[g])
        pivot_row = pivot_row * inv
        unit = unit * inv
        for h in range(g, groups):
            factor = jnp.broadcast_to(left[h][:, j:j + 1], (8, n))
            if h == g:
                factor = jnp.where(row_id > i, factor, 0.0)
            left[h] = left[h] - factor * pivot_row
            right[h] = right[h] - factor * unit
    return jnp.concatenate(done, axis=0)


def local_kernel(
    rows_each, merged_ref, mean_ref, gram_ref, full_ref, weights_ref, momentum_ref,
    error_out, weights_out, momentum_out, own_ref,
):
    me = lax.axis_index("rep")
    gram = gram_ref[...]
    first = full_ref[...]
    reached = dot(gram, first, NN)
    lower_inv = inverse_factor(dot(first, reached, TN))
    right = dot(reached, lower_inv, NT)
    reached = dot(gram, right, NN)
    lower_inv = inverse_factor(dot(right, reached, TN))
    to_left = dot(right, lower_inv, NT)
    right = dot(reached, lower_inv, NT)
    left = dot(mean_ref[...], to_left, NN)
    own_ref[...] = left
    error_out[0] = merged_ref[...] - dot(left, right, NT)
    mine = own_ref[pl.ds(pl.multiple_of(me * rows_each, rows_each), rows_each), :]
    approx = dot(mine, right, NT)
    momentum = MOMENTUM * momentum_ref[0] + approx
    momentum_out[0] = momentum
    weights_out[0] = weights_ref[0] - RATE * (approx + MOMENTUM * momentum)


def on_device(nx, ny, nz, tokens_in, norm_gain, key_grad, error_in, basis_init, weights_in, momentum_in):
    tok, dl = tokens_in.shape
    kw = key_grad.shape[1]
    rank = basis_init.shape[1]
    half, ghalf = dl // 2, kw // 2
    rp, gp = half // (nx * ny), ghalf // (nx * ny)
    vmem = pl.BlockSpec(memory_space=pltpu.VMEM)
    anywhere = pl.BlockSpec(memory_space=pl.ANY)
    big = max(nx, ny)
    copies = 3 * nz + 2 + 2 * big + 1 + 2 * big + 2 * big + 2 * big + 2
    V = pltpu.VMEM
    merged, mean, gram, full = pl.pallas_call(
        functools.partial(exchange_kernel, nx, ny, nz),
        out_shape=[
            jax.ShapeDtypeStruct((dl, kw), F32),
            jax.ShapeDtypeStruct((dl, kw), F32),
            jax.ShapeDtypeStruct((kw, kw), F32),
            jax.ShapeDtypeStruct((kw, rank), F32),
        ],
        in_specs=[anywhere, vmem, anywhere, anywhere, vmem],
        out_specs=[anywhere, vmem, vmem, vmem],
        scratch_shapes=[
            V((tok, dl), jnp.bfloat16),
            V((tok, kw), jnp.bfloat16),
            V((dl, kw), F32),
            V((tok, dl), jnp.bfloat16),
            V((dl, kw), F32),
            V((half, kw), F32),
            V((half, kw), F32),
            V((nz, 1, tok), F32),
            V((nx, ny * rp, kw), F32),
            V((ny, rp, kw), F32),
            V((ny, nx * rp, kw), F32),
            V((nx, rp, kw), F32),
            V((big * rp, kw), F32),
            V((2, rp, kw), F32),
            V((ghalf, kw), F32),
            V((nx, ny * gp, kw), F32),
            V((ny, gp, kw), F32),
            V((ny, nx * gp, kw), F32),
            V((nx, gp, kw), F32),
            V((big * gp, kw), F32),
            V((nz, gp, kw), F32),
            pltpu.SemaphoreType.DMA((4,)),
            pltpu.SemaphoreType.DMA((copies,)),
            pltpu.SemaphoreType.DMA((copies,)),
        ],
        compiler_params=pltpu.CompilerParams(
            collective_id=0, has_side_effects=True, vmem_limit_bytes=48 * 1024 * 1024
        ),
        name="exchange",
    )(tokens_in, norm_gain.reshape(1, dl), key_grad, error_in, basis_init)
    rows_each = weights_in.shape[1]
    return pl.pallas_call(
        functools.partial(local_kernel, rows_each),
        out_shape=[
            jax.ShapeDtypeStruct((1, dl, kw), F32),
            jax.ShapeDtypeStruct(weights_in.shape, F32),
            jax.ShapeDtypeStruct(momentum_in.shape, F32),
        ],
        in_specs=[vmem] * 6,
        out_specs=[vmem] * 3,
        scratch_shapes=[V((dl, rank), F32)],
        compiler_params=pltpu.CompilerParams(vmem_limit_bytes=48 * 1024 * 1024),
        name="local",
    )(merged, mean, gram, full, weights_in, momentum_in)


def solution(mesh):
    nz = mesh.shape["mp"]
    nx, ny = SHAPE if mesh.shape["rep"] == 64 else (2, mesh.shape["rep"] // 4)
    in_specs = (
        P("rep", "mp"),
        P("mp"),
        P("rep", None),
        P("rep", "mp", None),
        P("mp", None),
        P("mp", "rep", None),
        P("mp", "rep", None),
    )
    out_specs = (P("rep", "mp", None), P("mp", "rep", None), P("mp", "rep", None))
    return jax.shard_map(
        functools.partial(on_device, nx, ny, nz),
        mesh=mesh, in_specs=in_specs, out_specs=out_specs, check_vma=False,
    )
```

```python
import functools

import jax
import jax.numpy as jnp
from jax import lax
from jax.experimental import pallas as pl
from jax.experimental.pallas import tpu as pltpu
from jax.sharding import PartitionSpec as P

D = 8192
CORES = 2
SHAPE = (4, 8)
MESH = pl.DeviceIdType.MESH
F32 = jnp.float32
HI = lax.Precision.HIGHEST
EPS = 1e-5
MOMENTUM = 0.9
RATE = 0.7


def dot(a, b, dims, precision=HI):
    return lax.dot_general(a, b, (dims, ((), ())), precision=precision, preferred_element_type=F32)


NN = ((1,), (0,))
TN = ((0,), (0,))
NT = ((1,), (1,))
ITERS = 2
UPPER = ((0, 0), (0, 1), (0, 2), (0, 3), (1, 1), (1, 2), (1, 3), (2, 2), (2, 3), (3, 3))


def split_dot(a, b, dims):
    def parts(v):
        high = v.astype(jnp.bfloat16)
        return high, (v - high.astype(F32)).astype(jnp.bfloat16)

    (ah, al), (bh, bl) = parts(a), parts(b)
    return dot(ah, bh, dims, None) + (dot(ah, bl, dims, None) + dot(al, bh, dims, None))


def exchange_kernel(
    nx, ny, nz,
    tok_h, gain_h, kg_h, err_h, basis_h,
    merged_h, left_ref, right_ref,
    mean_ref, gram_ref, cur, to_left, gain_ref, basis_ref,
    tok, kg, err, nrm, mg, cx, hs,
    sq, m0d, m0u, m0b, m1d, m1u, m1b, part, rows, gtri,
    gh0, g0a, g0b, gpart0, gz0, gh1, g1a, g1b, gpart1, gz1,
    local_sem, ssem, rsem,
):
    me = lax.axis_index("rep")
    z = lax.axis_index("mp")
    core = lax.rem(me, 2)
    y = lax.rem(lax.div(me, 2), ny)
    x = lax.div(me, 2 * ny)
    reps = nx * ny * CORES
    dl, kw = mg.shape
    half = dl // 2

    def at(xx, yy, cc, zz):
        return ((xx * ny + yy) * 2 + cc, zz)

    partner = at(x, y, 1 - core, z)
    xs = [None] + [at(lax.rem(x + d, nx), y, core, z) for d in range(1, nx)]
    ys = [None] + [at(x, lax.rem(y + d, ny), core, z) for d in range(1, ny)]
    zs = [None] + [at(x, y, core, lax.rem(z + d, nz)) for d in range(1, nz)]

    loads = [
        pltpu.make_async_copy(tok_h, tok, local_sem.at[0]),
        pltpu.make_async_copy(kg_h, kg, local_sem.at[1]),
        pltpu.make_async_copy(err_h.at[0], err, local_sem.at[2]),
        pltpu.make_async_copy(gain_h, gain_ref, local_sem.at[4]),
        pltpu.make_async_copy(basis_h, basis_ref, local_sem.at[5]),
    ]
    for load in loads:
        load.start()
    barrier = pltpu.get_barrier_semaphore()
    peers = [partner] + xs[1:] + ys[1:] + zs[1:]
    for peer in peers:
        pl.semaphore_signal(barrier, inc=1, device_id=peer, device_id_type=MESH)

    count = [0]

    def ids(n):
        first = count[0]
        count[0] += n
        return first

    def copy(src, dst, k, dev):
        return pltpu.make_async_remote_copy(
            src_ref=src, dst_ref=dst, send_sem=ssem.at[k], recv_sem=rsem.at[k], device_id=dev, device_id_type=MESH
        )

    def start(copies):
        for c in copies:
            c.start()

    def arrive(copies):
        for c in copies:
            c.wait_recv()

    def sent(copies):
        for c in copies:
            c.wait_send()

    loads[0].wait()
    acc = jnp.zeros((tok.shape[0], 128), F32)
    for b in range(dl // 128):
        t = tok[:, b * 128:(b + 1) * 128].astype(F32)
        acc = acc + t * t
    sq[0] = jnp.sum(acc.T, axis=0, keepdims=True)
    zb = basis_ref.shape[0]
    loads[4].wait()
    mine = cur.at[pl.ds(pl.multiple_of(z * zb, zb), zb), :]
    mine[...] = basis_ref[...]
    pl.semaphore_wait(barrier, len(peers))

    k = ids(nz)
    sq_copies = [copy(sq.at[0], sq.at[d], k + d, zs[d]) for d in range(1, nz)]
    start(sq_copies)
    arrive(sq_copies)
    total = sq[0]
    for d in range(1, nz):
        total = total + sq[d]
    scale = lax.rsqrt(total / D + EPS)
    scale = jnp.broadcast_to(scale, (128, scale.shape[1])).T
    loads[3].wait()
    for b in range(dl // 128):
        cols = slice(b * 128, (b + 1) * 128)
        t = tok[:, cols].astype(F32) * scale * gain_ref[:, cols].astype(F32)
        nrm[:, cols] = t.astype(jnp.bfloat16)
    loads[1].wait()
    loads[2].wait()

    step = half // 4
    k = ids(4)
    pair_copies = []
    turn_x, turn_y = x, lax.div(y * 4, ny)

    def quarter(owner, m):
        turn = jnp.where(owner == 0, turn_x, turn_y)
        return pl.multiple_of(lax.rem(turn + (2, 1, 3, 0)[m], 4) * step, step)

    def merge(first):
        first = pl.multiple_of(first, step)
        w = dot(nrm[:, pl.ds(first, step)], kg[...], TN, None)
        mg[pl.ds(first, step), :] = w + err[pl.ds(first, step), :]

    for m in range(4):
        low = quarter(1 - core, m)
        first = pl.multiple_of((1 - core) * half + low, step)
        merge(first)
        c = copy(mg.at[pl.ds(first, step), :], cx.at[pl.ds(low, step), :], k + m, partner)
        c.start()
        pair_copies.append(c)
    for m in range(4):
        merge(core * half + quarter(core, m))

    def ready(m):
        low = quarter(core, m)
        pair_copies[m].wait_recv()
        own = pl.ds(pl.multiple_of(core * half + low, step), step)
        hs[pl.ds(low, step), :] = mg[own, :] + cx[pl.ds(low, step), :]

    k = ids(nz)
    basis_copies = [copy(basis_ref, mine, k + d, zs[d]) for d in range(1, nz)]
    start(basis_copies)
    store = pltpu.make_async_copy(mg, merged_h, local_sem.at[3])
    store.start()
    def scatter(src, base, size, slots, peers, place, n, k):
        out = []
        for d in range(1, n):
            target = lax.rem(place + d, n)
            first = pl.multiple_of(base + target * size, size)
            out.append(copy(src.at[pl.ds(first, size), :], slots.at[d], k + d, peers[d]))
        return out

    def gathered(src, base, size, slots, place, n):
        v = src[pl.ds(pl.multiple_of(base + place * size, size), size), :]
        for d in range(1, n):
            v = v + slots[d]
        return v

    big = max(nx, ny)
    ka, kb = ids((big + 2) * 4), ids(big)
    rp = half // (nx * ny)
    row = pl.multiple_of(jnp.where(core == 0, (x * ny + y) * rp, half + (y * nx + x) * rp), rp)

    def ring(src, size, subs, down, up, low, high, place, n, k, needs):
        hops = n // 2
        sub = size // subs

        def own(t, q):
            first = lax.rem(t + 2 * n, n) * size + q * sub
            return pl.ds(pl.multiple_of(first, sub), sub)

        moved = {}
        for s in range(1, hops + 1):
            for m in needs.get(s, ()):
                ready(m)
            for q in range(subs):
                piece = pl.ds(q * sub, sub)
                sides = [(0, down, low, place - (hops - s + 1))]
                if s < hops:
                    sides.append((1, up, high, place + hops - s))
                for side, slots, peer, t in sides:
                    if s == 1:
                        source = src.at[own(t, q), :]
                    else:
                        moved[side, s - 1, q].wait_recv()
                        source = slots.at[s - 1, piece, :]
                        slots[s - 1, piece, :] = slots[s - 1, piece, :] + src[own(t, q), :]
                    c = copy(source, slots.at[s, piece, :], k + (s * 2 + side) * subs + q, peer)
                    c.start()
                    moved[side, s, q] = c
        last = (src[pl.ds(pl.multiple_of(place * size, size), size), :],)
        for q in range(subs):
            moved[0, hops, q].wait_recv()
            moved[1, hops - 1, q].wait_recv()
        total = last[0] + down[hops] + up[hops - 1]
        return total, list(moved.values())

    def plane(src, part, slots0, slots1, b0, b1, piece, subs, ka, kb, put):
        @pl.when(core == 0)
        def _():
            total, first = ring(src, ny * piece, subs, slots0[0], slots0[1], xs[nx - 1], xs[1], x, nx, ka, {1: (0, 1), 2: (2, 3)})
            part[pl.ds(0, ny * piece), :] = total
            second = scatter(part, 0, piece, b0, ys, y, ny, kb)
            start(second)
            arrive(second)
            put(gathered(part, 0, piece, b0, y, ny))
            sent(first)
            sent(second)

        @pl.when(core == 1)
        def _():
            total, first = ring(src, nx * piece, subs, slots1[0], slots1[1], ys[ny - 1], ys[1], y, ny, ka, {1: (0, 1), 2: (2,), 3: (3,)})
            part[pl.ds(0, nx * piece), :] = total
            second = scatter(part, 0, piece, b1, xs, x, nx, kb)
            start(second)
            arrive(second)
            put(gathered(part, 0, piece, b1, x, nx))
            sent(first)
            sent(second)

    def put_rows(v):
        v = v * (1.0 / reps)
        mean_ref[pl.ds(row, rp), :] = v
        rows[0] = v

    plane(hs, part, (m0d, m0u), (m1d, m1u), m0b, m1b, rp, 4, ka, kb, put_rows)

    k = ids(1)
    row_copy = copy(rows.at[0], rows.at[1], k, partner)
    row_copy.start()

    def spread(ref, base0, base1, piece, ka, kb):
        def block(first, size):
            return ref.at[pl.ds(pl.multiple_of(first, size), size), :]

        def along(first, size, peers, n, k):
            if first is None:
                return []
            return [copy(block(first, size), block(first, size), k + d, peers[d]) for d in range(1, n)]

        def place(base, index):
            return None if base is None else base + index * piece

        one0 = along(place(base0, x * ny + y), piece, ys, ny, ka)
        two0 = along(place(base0, x * ny), ny * piece, xs, nx, kb)
        one1 = along(place(base1, y * nx + x), piece, xs, nx, ka)
        two1 = along(place(base1, y * nx), nx * piece, ys, ny, kb)
        return one0, two0, one1, two1

    def by_core(zero, one, act):
        @pl.when(core == 0)
        def _():
            act(zero)

        @pl.when(core == 1)
        def _():
            act(one)

    mean_one0, mean_two0, mean_one1, mean_two1 = spread(mean_ref, 0, half, rp, ids(big), ids(big))
    by_core(mean_one0, mean_one1, start)

    row_copy.wait_recv()
    both = rows[...].reshape(2 * rp, kw)
    tile = kw // 4
    tiles = [both[:, i * tile:(i + 1) * tile] for i in range(4)]
    gp0, gp1 = 6 * tile // (nx * ny), 4 * tile // (nx * ny)
    gbase1 = 6 * tile

    def direct(src, part, a, b, first, second, piece, ka, kb):
        (peers1, place1, n1), (peers2, place2, n2) = first, second
        one = scatter(src, 0, n2 * piece, a, peers1, place1, n1, ka)
        start(one)
        arrive(one)
        part[...] = gathered(src, 0, n2 * piece, a, place1, n1)
        two = scatter(part, 0, piece, b, peers2, place2, n2, kb)
        start(two)
        arrive(two)
        v = gathered(part, 0, piece, b, place2, n2)
        sent(one)
        sent(two)
        return v

    ka, kb = ids(big), ids(big)

    @pl.when(core == 0)
    def _():
        for j, (i, k) in enumerate(UPPER[:6]):
            gh0[j * tile:(j + 1) * tile, :] = dot(tiles[i], tiles[k], TN)
        gz0[0] = direct(gh0, gpart0, g0a, g0b, (xs, x, nx), (ys, y, ny), gp0, ka, kb)

    @pl.when(core == 1)
    def _():
        for j, (i, k) in enumerate(UPPER[6:]):
            gh1[j * tile:(j + 1) * tile, :] = dot(tiles[i], tiles[k], TN)
        gz1[0] = direct(gh1, gpart1, g1a, g1b, (ys, y, ny), (xs, x, nx), gp1, ka, kb)

    k = ids(nz)
    z_zero = [copy(gz0.at[0], gz0.at[d], k + d, zs[d]) for d in range(1, nz)]
    z_one = [copy(gz1.at[0], gz1.at[d], k + d, zs[d]) for d in range(1, nz)]
    by_core(z_zero, z_one, start)
    by_core(mean_one0, mean_one1, arrive)

    def near(copies):
        n = len(copies)
        return [c for i, c in enumerate(copies) if min(i, n - 1 - i) < n // 4 + 1]

    def far(copies):
        close = near(copies)
        return [c for c in copies if all(c is not o for o in close)]

    by_core(near(mean_two0), near(mean_two1), start)
    by_core(z_zero, z_one, arrive)

    def over_z(ref, base, piece, index):
        v = ref[0]
        for d in range(1, nz):
            v = v + ref[d]
        gtri[pl.ds(pl.multiple_of(base + index * piece, 8), piece), :] = v

    @pl.when(core == 0)
    def _():
        over_z(gz0, 0, gp0, x * ny + y)

    @pl.when(core == 1)
    def _():
        over_z(gz1, gbase1, gp1, y * nx + x)

    ka, kb = ids(big), ids(big)
    gram_one0, gram_two0, _, _ = spread(gtri, 0, None, gp0, ka, kb)
    _, _, gram_one1, gram_two1 = spread(gtri, None, gbase1, gp1, ka, kb)
    by_core(gram_one0, gram_one1, start)
    by_core(gram_one0, gram_one1, arrive)
    by_core(gram_two0, gram_two1, start)
    by_core(gram_two0, gram_two1, arrive)
    k = ids(2)
    six, four = gtri.at[pl.ds(0, 6 * tile), :], gtri.at[pl.ds(gbase1, 4 * tile), :]
    swap_zero = [copy(six, six, k, partner)]
    swap_one = [copy(four, four, k + 1, partner)]
    by_core(swap_zero, swap_one, start)
    by_core(far(mean_two0), far(mean_two1), start)
    arrive(basis_copies)
    by_core(swap_one, swap_zero, arrive)
    for j, (i, k) in enumerate(UPPER):
        v = gtri[j * tile:(j + 1) * tile, :]
        gram_ref[i * tile:(i + 1) * tile, k * tile:(k + 1) * tile] = v
        if i != k:
            gram_ref[k * tile:(k + 1) * tile, i * tile:(i + 1) * tile] = v.T

    def iterate(step, carry):
        reached = dot(gram_ref[...], cur[...], NN)
        lower_inv = inverse_factor(dot(cur[...], reached, TN))

        @pl.when(step == ITERS - 1)
        def _():
            to_left[...] = dot(cur[...], lower_inv, NT)

        cur[...] = dot(reached, lower_inv, NT)
        return carry

    lax.fori_loop(0, ITERS, iterate, 0)
    by_core(mean_two0, mean_two1, arrive)
    own = pl.ds(pl.multiple_of(core * half, half), half)
    left_ref[own, :] = split_dot(mean_ref[own, :], to_left[...], NN)
    own = left_ref.at[own, :]
    left_swap = copy(own, own, ids(1), partner)
    left_swap.start()
    right_ref[...] = cur[...]
    store.wait()
    left_swap.wait()
    sent(sq_copies + basis_copies + pair_copies + [row_copy])
    by_core(z_zero, z_one, sent)
    by_core(swap_zero, swap_one, sent)
    by_core(mean_one0, mean_one1, sent)
    by_core(mean_two0, mean_two1, sent)
    by_core(gram_one0, gram_one1, sent)
    by_core(gram_two0, gram_two1, sent)


def lane(v, j):
    return jnp.broadcast_to(v[:, j:j + 1], v.shape)


def row(v, i):
    return jnp.broadcast_to(v[i:i + 1, :], v.shape)


def inverse_factor(a):
    n = a.shape[0]
    groups = n // 8
    rows = [a[8 * g:8 * g + 8, :] for g in range(groups)]
    row_id = lax.broadcasted_iota(jnp.int32, (8, n), 0)
    lane_id = lax.broadcasted_iota(jnp.int32, (8, n), 1)
    here = [row_id == i for i in range(8)]
    result = []
    for g in range(groups):
        block = (lane_id >= 8 * g) & (lane_id < 8 * g + 8)
        unit = jnp.where(lane_id == row_id + 8 * g, 1.0, 0.0).astype(F32)
        columns = [lane(rows[g], 8 * g + i) for i in range(8)]
        top = jnp.where(block, unit, rows[g])
        out = top
        for i in range(8):
            pivot = row(columns[i], i)
            inv = 1.0 / pivot
            coeff = jnp.where(here[i], -1.0, columns[i])

            def eliminate(v):
                return jnp.where(here[i], 0.0, v) - coeff * (row(v, i) * inv)

            out = jnp.where(here[i], top * lax.rsqrt(pivot), out)
            for k in range(i + 1, 8):
                columns[k] = eliminate(columns[k])
            top = eliminate(top)
        result.append(jnp.where(lane_id < 8 * g + 8, out, 0.0))
        tops = [row(top, i) for i in range(8)]
        for h in range(g + 1, groups):
            p = [lane(rows[h], 8 * g + i) * tops[i] for i in range(8)]
            p = ((p[0] + p[1]) + (p[2] + p[3])) + ((p[4] + p[5]) + (p[6] + p[7]))
            rows[h] = jnp.where(block, 0.0, rows[h]) - p
    return jnp.concatenate(result, axis=0)


def output_kernel(
    rows_each, merged_ref, left_ref, right_ref, weights_ref, momentum_ref,
    error_h, weights_out, momentum_out, error, sem,
):
    block = error.shape[1]
    stores = []
    for i in range(error.shape[0]):
        here = slice(i * block, (i + 1) * block)
        error[i] = merged_ref[here, :] - split_dot(left_ref[here, :], right_ref[...], NT)
        stores.append(pltpu.make_async_copy(error.at[i], error_h.at[0, pl.ds(i * block, block), :], sem.at[i]))
        stores[i].start()
    first = lax.axis_index("rep") * rows_each
    approx = split_dot(left_ref[pl.ds(pl.multiple_of(first, rows_each), rows_each), :], right_ref[...], NT)
    momentum = MOMENTUM * momentum_ref[0] + approx
    momentum_out[0] = momentum
    weights_out[0] = weights_ref[0] - RATE * (approx + MOMENTUM * momentum)
    for store in stores:
        store.wait()


def on_device(nx, ny, nz, tokens_in, norm_gain, key_grad, error_in, basis_init, weights_in, momentum_in):
    tok, dl = tokens_in.shape
    kw = key_grad.shape[1]
    rank = basis_init.shape[1]
    half, tile = dl // 2, kw // 4
    rp, gp0, gp1 = half // (nx * ny), 6 * tile // (nx * ny), 4 * tile // (nx * ny)
    vmem = pl.BlockSpec(memory_space=pltpu.VMEM)
    anywhere = pl.BlockSpec(memory_space=pl.ANY)
    big = max(nx, ny)
    copies = 3 * nz + 10 + 4 * (big + 2) + 8 * big
    V = pltpu.VMEM
    keep = lambda v: pltpu.with_memory_space_constraint(v, pltpu.HBM)
    merged, left, right = pl.pallas_call(
        functools.partial(exchange_kernel, nx, ny, nz),
        out_shape=[
            jax.ShapeDtypeStruct((dl, kw), F32),
            jax.ShapeDtypeStruct((dl, rank), F32),
            jax.ShapeDtypeStruct((kw, rank), F32),
        ],
        in_specs=[pl.BlockSpec(memory_space=pltpu.HBM)] * 5,
        out_specs=[anywhere, vmem, vmem],
        scratch_shapes=[
            V((dl, kw), F32),
            V((kw, kw), F32),
            V((kw, rank), F32),
            V((kw, rank), F32),
            V((1, dl), jnp.bfloat16),
            V(basis_init.shape, F32),
            V((tok, dl), jnp.bfloat16),
            V((tok, kw), jnp.bfloat16),
            V((dl, kw), F32),
            V((tok, dl), jnp.bfloat16),
            V((dl, kw), F32),
            V((half, kw), F32),
            V((half, kw), F32),
            V((nz, 1, tok), F32),
            V((nx // 2 + 1, ny * rp, kw), F32),
            V((nx // 2 + 1, ny * rp, kw), F32),
            V((ny, rp, kw), F32),
            V((ny // 2 + 1, nx * rp, kw), F32),
            V((ny // 2 + 1, nx * rp, kw), F32),
            V((nx, rp, kw), F32),
            V((big * rp, kw), F32),
            V((2, rp, kw), F32),
            V((10 * tile, tile), F32),
            V((6 * tile, tile), F32),
            V((nx, ny * gp0, tile), F32),
            V((ny, gp0, tile), F32),
            V((ny * gp0, tile), F32),
            V((nz, gp0, tile), F32),
            V((4 * tile, tile), F32),
            V((ny, nx * gp1, tile), F32),
            V((nx, gp1, tile), F32),
            V((nx * gp1, tile), F32),
            V((nz, gp1, tile), F32),
            pltpu.SemaphoreType.DMA((6,)),
            pltpu.SemaphoreType.DMA((copies,)),
            pltpu.SemaphoreType.DMA((copies,)),
        ],
        compiler_params=pltpu.CompilerParams(
            collective_id=0, has_side_effects=True, vmem_limit_bytes=48 * 1024 * 1024
        ),
        name="exchange",
    )(keep(tokens_in), norm_gain.reshape(1, dl), keep(key_grad), keep(error_in), keep(basis_init))
    rows_each = weights_in.shape[1]
    steps = 8
    return pl.pallas_call(
        functools.partial(output_kernel, rows_each),
        out_shape=[
            jax.ShapeDtypeStruct((1, dl, kw), F32),
            jax.ShapeDtypeStruct(weights_in.shape, F32),
            jax.ShapeDtypeStruct(momentum_in.shape, F32),
        ],
        in_specs=[vmem] * 5,
        out_specs=[anywhere, vmem, vmem],
        scratch_shapes=[V((steps, dl // steps, kw), F32), pltpu.SemaphoreType.DMA((steps,))],
        compiler_params=pltpu.CompilerParams(vmem_limit_bytes=24 * 1024 * 1024),
        name="outputs",
    )(merged, left, right, weights_in, momentum_in)


def solution(mesh):
    nz = mesh.shape["mp"]
    nx, ny = SHAPE if mesh.shape["rep"] == 64 else (2, mesh.shape["rep"] // 4)
    in_specs = (
        P("rep", "mp"),
        P("mp"),
        P("rep", None),
        P("rep", "mp", None),
        P("mp", None),
        P("mp", "rep", None),
        P("mp", "rep", None),
    )
    out_specs = (P("rep", "mp", None), P("mp", "rep", None), P("mp", "rep", None))
    return jax.shard_map(
        functools.partial(on_device, nx, ny, nz),
        mesh=mesh, in_specs=in_specs, out_specs=out_specs, check_vma=False,
    )
```
